128 devices in a mesh: rows: 128 (over z, y, x, core).
Axes of the slice: x: 4, y: 4, z: 4, core: 2. Of those that a mesh axis runs over, the one named last changes fastest.
Arguments:
- edge_tiles: bfloat16 [32768, 128, 128], P('rows'), may hold values from -0.5 to 0.5
- tile_row: int32 [32768], P('rows'), may hold values from 0 to 7
- tile_slot: int32 [32768], P('rows'), may hold values from 0 to 255, as said below
- tile_count: int32 [128], P('rows'), may hold values from 32 to 256, as said below
- fetch_list: int32 [128, 256], P('rows'), may hold values from 0 to 7, as said below
- hub_start: float32 [8, 131072], P(None, 'rows'), may hold values from -6 to 6
Outputs:
- hub: float32 [8, 131072], P(None, 'rows')
- authority: float32 [8, 131072], P(None, 'rows')
The draws below stay inside these ranges and needn't reach their ends.
Inputs may be any that keep to these rules, and one draw needn't show every extreme that they name: tile_slot[t] = p * 2 + k names entry k of the fetch_list group of device p, in the row of the tile's own device. `fetch_list`: entries p * 2 to p * 2 + 1 of each row are 2 distinct block numbers among device p's own 8 blocks. Tile slots of device d at positions 256 * d + i with i >= tile_count[d] are not part of the graph.
All inputs are finite; a program needn't handle non-finite values.
Results may differ from the reference program's by a relative error of at most 0.004.
Values may be sent and summed in bfloat16 or wider, within the bound.
A program may use at most 64 MiB of HBM per device.

```python
import jax
import jax.numpy as jnp
from jax import lax

TILE = 128
COLS = 8
BLK_DEV = 8
TILES_DEV = 256
SLOTS = 2
ITERS = 2
NODES = 131072
TILES = 32768
N_ROWS = 128


def draw_tile_slot(key, part):
    owner_ids = jnp.arange(N_ROWS, dtype=jnp.int32)
    weights = N_ROWS + 3 * owner_ids
    cumulative = jnp.cumsum(weights).astype(jnp.int32)
    key_owner, key_entry = jax.random.split(jax.random.fold_in(key, 11))
    picks = jax.random.randint(key_owner, (TILES_DEV * N_ROWS,), 0, cumulative[N_ROWS - 1], dtype=jnp.int32)
    owners = jnp.searchsorted(cumulative, picks, side='right').astype(jnp.int32)
    entries = jax.random.randint(key_entry, (TILES_DEV * N_ROWS,), 0, SLOTS, dtype=jnp.int32)
    return (owners * SLOTS + entries).astype(jnp.int32)


def draw_tile_count(key, part):
    position = jnp.arange(N_ROWS, dtype=jnp.int32)
    lowest = TILES_DEV // 8
    extent = TILES_DEV - lowest
    divisor = max(N_ROWS - 1, 1)
    rising = lowest + extent * position * position // (divisor * divisor)
    jitter_term = jax.random.randint(jax.random.fold_in(key, 23), (N_ROWS,), -(TILES_DEV // 16), TILES_DEV // 16 + 1, dtype=jnp.int32)
    counted = jnp.clip(rising + jitter_term, lowest, TILES_DEV)
    return counted.at[N_ROWS - 1].set(TILES_DEV).astype(jnp.int32)


def draw_fetch_list(key, part):
    scores = jax.random.randint(jax.random.fold_in(key, 37), (N_ROWS, N_ROWS, BLK_DEV), 0, 1 << 20, dtype=jnp.int32)
    ordering = jnp.argsort(scores, axis=-1, stable=True)[:, :, :SLOTS]
    return ordering.reshape(N_ROWS, N_ROWS * SLOTS).astype(jnp.int32)


def place_ends(values, own_key, least, high):
    longest = values.shape.index(max(values.shape))
    spots = []
    for shift in (0, 1):
        where = [jax.random.randint(jax.random.fold_in(own_key, axis), (), 0, length) for axis, length in enumerate(values.shape)]
        where[longest] = (where[longest] + shift) % values.shape[longest]
        spots.append(tuple(where))
    return values.at[spots[0]].set(least).at[spots[1]].set(high)


def block_scale(key, dims, shards, least, high):
    factor_of = 1.0
    for axis_at, shards_of in shards:
        heights = jax.random.uniform(jax.random.fold_in(jax.random.fold_in(key, 6), axis_at), (shards_of,), jnp.float32, least / len(shards), high / len(shards))
        factor_of = factor_of * jnp.repeat(jnp.exp(heights), dims[axis_at] // shards_of).reshape((-1,) + (1,) * (len(dims) - 1 - axis_at))
    return factor_of


def scatter_about(rng, shape, width, most, cuts=(), kind=jnp.bfloat16):
    gain = block_scale(rng, shape, cuts, -0.22, 0.18) if cuts else 1.0
    array = jax.random.normal(rng, shape, jnp.float32) * width * gain
    return jnp.minimum(jnp.maximum(array, -most), most).astype(kind)


def setup_inputs(seed: int = 0) -> dict:
    keys = jax.random.split(jax.random.key(seed), 7)
    return {
        "edge_tiles": scatter_about(keys[0], (TILES, TILE, TILE), TILE ** -0.5, 0.5, ((0, 128),)),
        "tile_row": place_ends(jax.random.randint(keys[1], (TILES,), 0, BLK_DEV), jax.random.fold_in(keys[1], 1), 0, BLK_DEV - 1).astype(jnp.int32),
        "tile_slot": draw_tile_slot(jax.random.fold_in(keys[6], 71), 0),
        "tile_count": draw_tile_count(jax.random.fold_in(keys[6], 71), 0),
        "fetch_list": draw_fetch_list(jax.random.fold_in(keys[6], 71), 0),
        "hub_start": scatter_about(keys[5], (COLS, NODES), 1.0, 6.0, ((1, 128),), jnp.float32),
    }


def column_scale(raw_blocks):
    mean_square = lax.optimization_barrier(jnp.sum(raw_blocks * raw_blocks, axis=(0, 2))) / (BLK_DEV * N_ROWS * TILE)
    return raw_blocks / jnp.sqrt(mean_square + 1e-06)[None, :, None]

def reference(edge_tiles, tile_row, tile_slot, tile_count, fetch_list, hub_start):
    blocks = BLK_DEV * N_ROWS
    tiles_split = edge_tiles.reshape(N_ROWS, TILES_DEV, TILE, TILE)
    rows_split = tile_row.reshape(N_ROWS, TILES_DEV).astype(jnp.int32)
    slots_split = tile_slot.reshape(N_ROWS, TILES_DEV).astype(jnp.int32)
    device_ids = jnp.arange(N_ROWS, dtype=jnp.int32)

    def placement(rows_here, slots_here, count_here, fetch_here, device):
        rows_global = device * BLK_DEV + rows_here
        owners = slots_here // SLOTS
        cols_global = owners * BLK_DEV + jnp.take(fetch_here, slots_here).astype(jnp.int32)
        alive_mask = (jnp.arange(TILES_DEV, dtype=jnp.int32) < count_here).astype(jnp.float32)
        return (rows_global, cols_global, alive_mask)

    def transpose_pass(hub_low):

        def per_device(running, inputs):
            tiles_here, rows_here, slots_here, count_here, fetch_here, device = inputs
            rows_global, cols_global, alive_mask = placement(rows_here, slots_here, count_here, fetch_here, device)
            source = jnp.take(hub_low, rows_global, axis=0).astype(jnp.float32)
            product = jnp.einsum('gce,gef->gcf', source, tiles_here.astype(jnp.float32), precision=lax.Precision.HIGHEST)
            product = product * alive_mask[:, None, None]
            return (running + jax.ops.segment_sum(product, cols_global, num_segments=blocks), None)
        start_value = jnp.zeros((blocks, COLS, TILE), jnp.float32)
        running, _ = lax.scan(per_device, start_value, (tiles_split, rows_split, slots_split, tile_count.astype(jnp.int32), fetch_list.astype(jnp.int32), device_ids))
        return running

    def forward_pass(authority_low):

        def per_device(running, inputs):
            tiles_here, rows_here, slots_here, count_here, fetch_here, device = inputs
            rows_global, cols_global, alive_mask = placement(rows_here, slots_here, count_here, fetch_here, device)
            source = jnp.take(authority_low, cols_global, axis=0).astype(jnp.float32)
            product = jnp.einsum('gcf,gef->gce', source, tiles_here.astype(jnp.float32), precision=lax.Precision.HIGHEST)
            product = product * alive_mask[:, None, None]
            return (running + jax.ops.segment_sum(product, rows_global, num_segments=blocks), None)
        start_value = jnp.zeros((blocks, COLS, TILE), jnp.float32)
        running, _ = lax.scan(per_device, start_value, (tiles_split, rows_split, slots_split, tile_count.astype(jnp.int32), fetch_list.astype(jnp.int32), device_ids))
        return running
    hub_blocks = hub_start.reshape(COLS, blocks, TILE).transpose(1, 0, 2)
    hub_low = hub_blocks.astype(jnp.bfloat16)
    authority_blocks = hub_blocks
    for sweep in range(ITERS):
        authority_raw = transpose_pass(hub_low)
        authority_low = authority_raw.astype(jnp.bfloat16)
        hub_raw = forward_pass(authority_low)
        hub_blocks = column_scale(hub_raw)
        hub_low = hub_blocks.astype(jnp.bfloat16)
        authority_blocks = column_scale(authority_raw)
    hub = hub_blocks.transpose(1, 0, 2).reshape(COLS, blocks * TILE)
    authority = authority_blocks.transpose(1, 0, 2).reshape(COLS, blocks * TILE)
    return (hub, authority)
```

```python
import functools

import jax
import jax.numpy as jnp
from jax import lax
from jax.experimental import pallas as pl
from jax.experimental.pallas import tpu as pltpu
from jax.sharding import PartitionSpec as P

AXIS = "rows"
EPS = 1e-06
F32 = jnp.float32
BF16 = jnp.bfloat16
CHUNKS = 8
QUADS = 8
MESH = pl.DeviceIdType.MESH


def dot_nn(lhs, rhs):
    return lax.dot_general(lhs, rhs, (((1,), (0,)), ((), ())), preferred_element_type=F32)


def dot_nt(lhs, rhs):
    return lax.dot_general(lhs, rhs, (((1,), (1,)), ((), ())), preferred_element_type=F32)


def split_bf16(x):
    high = x.astype(BF16)
    return high, (x - high.astype(F32)).astype(BF16)


def iota(shape, dim):
    return lax.broadcasted_iota(jnp.int32, shape, dim)


def kernel(
    devices,
    node_total,
    rows_s,
    slots_s,
    count_s,
    tiles_hbm,
    rows_v,
    slots_v,
    fetch_v,
    hub_v,
    hub_out,
    auth_out,
    tiles,
    prod,
    stage,
    fetched,
    onehot_slot,
    pick_t,
    pick,
    src_a,
    src_b,
    src_al,
    src_bl,
    hub_stage,
    auth_stage,
    send,
    recv,
    recv_idx,
    send_sum,
    recv_sum,
    tile_sem,
    send_sem,
    recv_sem,
    idx_send_sem,
    idx_recv_sem,
    sum_send_sem,
    sum_recv_sem,
):
    tile_total, edge, _ = tiles.shape
    cols = hub_v.shape[0]
    blocks = hub_v.shape[1] // edge
    slots_total = fetch_v.shape[1]
    slots_each = slots_total // devices
    part = slots_each * cols
    me = lax.axis_index(AXIS)
    barrier = pltpu.get_barrier_semaphore()

    per_chunk = tile_total // CHUNKS
    for q in range(CHUNKS):
        window = pl.ds(q * per_chunk, per_chunk)
        pltpu.make_async_copy(tiles_hbm.at[window], tiles.at[window], tile_sem.at[q]).start()

    @pl.loop(1, devices)
    def _(s):
        pl.semaphore_signal(
            barrier, inc=1, device_id=(lax.rem(me + s, devices),), device_id_type=MESH
        )

    zero_block = jnp.zeros((cols, edge), F32)

    def set_source(blocks_f32, with_low):
        for b in range(blocks):
            x = blocks_f32(b)
            up = jnp.concatenate([x, zero_block], axis=0)
            down = jnp.concatenate([zero_block, x], axis=0)
            if with_low:
                src_a[b], src_al[b] = split_bf16(up)
                src_b[b], src_bl[b] = split_bf16(down)
            else:
                src_a[b] = up.astype(BF16)
                src_b[b] = down.astype(BF16)

    def store_quad(t, o):
        prod[pl.ds(t, cols, stride=tile_total), :] = o[:cols, :edge]
        prod[pl.ds(t + 1, cols, stride=tile_total), :] = o[cols : 2 * cols, :edge]
        prod[pl.ds(t + 2, cols, stride=tile_total), :] = o[2 * cols : 3 * cols, edge:]
        prod[pl.ds(t + 3, cols, stride=tile_total), :] = o[3 * cols :, edge:]

    def quad_lhs(a, b, t):
        r = [rows_s[t + q] for q in range(4)]
        return jnp.concatenate(
            [
                jnp.concatenate([a[r[0]], b[r[1]]], axis=1),
                jnp.concatenate([a[r[2]], b[r[3]]], axis=1),
            ],
            axis=0,
        )

    def transpose_tiles(first, total, with_low):
        def body(i, carry):
            for u in range(QUADS):
                t = first + (i * QUADS + u) * 4
                lhs = quad_lhs(src_a, src_b, t)
                if with_low:
                    lhs = jnp.concatenate([lhs, quad_lhs(src_al, src_bl, t)], axis=0)
                rhs = jnp.concatenate(
                    [
                        tiles[pl.ds(t, 2)].reshape(2 * edge, edge),
                        tiles[pl.ds(t + 2, 2)].reshape(2 * edge, edge),
                    ],
                    axis=1,
                )
                o = dot_nn(lhs, rhs)
                if with_low:
                    o = o[: 4 * cols] + o[4 * cols :]
                store_quad(t, o)
            return carry

        lax.fori_loop(0, total // (4 * QUADS), body, 0)

    def forward_tiles():
        def body(i, carry):
            for u in range(QUADS):
                t = (i * QUADS + u) * 4
                f = [fetched[slots_s[t + q]] for q in range(4)]
                lhs = jnp.concatenate(
                    [
                        jnp.concatenate([f[0], zero_block, f[2], zero_block], axis=0),
                        jnp.concatenate([zero_block, f[1], zero_block, f[3]], axis=0),
                    ],
                    axis=1,
                ).astype(BF16)
                rhs = jnp.concatenate(
                    [
                        jnp.concatenate([tiles[t], tiles[t + 1]], axis=1),
                        jnp.concatenate([tiles[t + 2], tiles[t + 3]], axis=1),
                    ],
                    axis=0,
                )
                store_quad(t, dot_nt(lhs, rhs))
            return carry

        lax.fori_loop(0, tile_total // (4 * QUADS), body, 0)

    def prod_split(c):
        return split_bf16(prod[c * tile_total : (c + 1) * tile_total, :])

    def scatter_to_slots(phase):
        chooser = onehot_slot[...]
        for c in range(cols):
            high, low = prod_split(c)
            total = dot_nn(chooser, high) + dot_nn(chooser, low)
            stage[pl.ds(c, slots_total, stride=cols), :] = total
        send[phase] = stage[...].astype(BF16).reshape(devices, part, edge)

    def exchange_start(phase):
        @pl.loop(1, devices)
        def _(s):
            d = lax.rem(me + s, devices)
            pltpu.make_async_remote_copy(
                src_ref=send.at[phase, d],
                dst_ref=recv.at[phase, me],
                send_sem=send_sem.at[phase],
                recv_sem=recv_sem.at[phase],
                device_id=(d,),
                device_id_type=MESH,
            ).start()

        recv[phase, me] = send[phase, me]

    def wait_bytes(ref, sem):
        others = ref.at[pl.ds(0, devices - 1)]
        pltpu.make_async_copy(others, others, sem).wait()

    def exchange_wait(phase):
        wait_bytes(recv.at[phase], recv_sem.at[phase])

    def sums_start(which, row):
        send_sum[which] = row

        @pl.loop(1, devices)
        def _(s):
            d = lax.rem(me + s, devices)
            pltpu.make_async_remote_copy(
                src_ref=send_sum.at[which],
                dst_ref=recv_sum.at[which, me],
                send_sem=sum_send_sem.at[which],
                recv_sem=sum_recv_sem.at[which],
                device_id=(d,),
                device_id_type=MESH,
            ).start()

        recv_sum[which, me] = row

    def sums_wait(which):
        wait_bytes(recv_sum.at[which], sum_recv_sem.at[which])
        return jnp.sum(recv_sum[which], axis=0)

    def to_row(column, offset):
        spot = iota((cols, edge), 1) == iota((cols, edge), 0) + offset
        return jnp.sum(jnp.where(spot, column, 0.0), axis=0, keepdims=True)

    def to_column(row, offset):
        spot = iota((cols, edge), 1) == iota((cols, edge), 0) + offset
        return jnp.sum(jnp.where(spot, row, 0.0), axis=1, keepdims=True)

    def combine(phase):
        arrived = recv[phase].reshape(slots_total * cols, edge)
        return dot_nn(pick[...], arrived)

    def reply(phase, authority):
        low = authority.astype(BF16)
        low = jnp.concatenate([low, jnp.zeros_like(low)], axis=0)
        answer = dot_nn(pick_t[...], low).astype(BF16)
        send[phase] = answer.reshape(devices, part, edge)

    def gather_rows():
        alive = iota((blocks, tile_total), 1) < count_s[0]
        chooser = jnp.where(
            alive & (rows_v[...] == iota((blocks, tile_total), 0)), 1.0, 0.0
        ).astype(BF16)
        for c in range(cols):
            high, low = prod_split(c)
            total = dot_nn(chooser, high) + dot_nn(chooser, low)
            hub_stage[pl.ds(c, blocks, stride=cols), :] = total

    def column_sums(ref):
        total = jnp.zeros((cols, edge), F32)
        for b in range(blocks):
            x = ref[b * cols : (b + 1) * cols, :]
            total = total + x * x
        return jnp.sum(total, axis=1, keepdims=True)

    def spread(phase):
        arrived = recv[phase].reshape(slots_total * cols, edge)
        fetched[...] = arrived.astype(F32).reshape(slots_total, cols, edge)

    set_source(lambda b: hub_v[:, b * edge : (b + 1) * edge], False)
    alive = iota((slots_total, tile_total), 1) < count_s[0]
    onehot_slot[...] = jnp.where(
        alive & (slots_v[...] == iota((slots_total, tile_total), 0)), 1.0, 0.0
    ).astype(BF16)
    for q in range(CHUNKS):
        window = pl.ds(q * per_chunk, per_chunk)
        pltpu.make_async_copy(tiles_hbm.at[window], tiles.at[window], tile_sem.at[q]).wait()
        transpose_tiles(q * per_chunk, per_chunk, False)
    pl.semaphore_wait(barrier, devices - 1)

    @pl.loop(1, devices)
    def _(s):
        d = lax.rem(me + s, devices)
        pltpu.make_async_remote_copy(
            src_ref=fetch_v,
            dst_ref=recv_idx.at[me],
            send_sem=idx_send_sem,
            recv_sem=idx_recv_sem,
            device_id=(d,),
            device_id_type=MESH,
        ).start()

    recv_idx[me] = fetch_v[...]
    scatter_to_slots(0)
    exchange_start(0)

    wait_bytes(recv_idx, idx_recv_sem)
    lists = recv_idx[...].reshape(devices, slots_total)
    lanes = iota((devices, slots_total), 1)
    columns = [
        jnp.broadcast_to(
            jnp.sum(
                jnp.where(lanes == me * slots_each + k, lists, 0).astype(F32),
                axis=1,
                keepdims=True,
            ),
            (devices, edge),
        )
        for k in range(slots_each)
    ]
    wide = slots_total * cols
    line = jnp.zeros((cols, wide), F32)
    tall = jnp.zeros((wide, edge), F32)
    for k in range(slots_each):
        j = iota((devices, wide), 1)
        p = iota((devices, wide), 0)
        expand = jnp.where((j // part == p) & ((j // cols) % slots_each == k), 1.0, 0.0)
        line = line + dot_nn(columns[k].T[:cols].astype(BF16), expand.astype(BF16))
        j = iota((wide, devices), 0)
        p = iota((wide, devices), 1)
        expand = jnp.where((j // part == p) & ((j // cols) % slots_each == k), 1.0, 0.0)
        tall = tall + dot_nn(expand.astype(BF16), columns[k].astype(BF16))
    line_blocks = line.astype(jnp.int32)
    same = iota((cols, wide), 1) % cols == iota((cols, wide), 0)
    for b in range(0, blocks, 2):
        pick[b * cols : (b + 2) * cols, :] = jnp.concatenate(
            [jnp.where((line_blocks == b + h) & same, 1.0, 0.0) for h in range(2)], axis=0
        ).astype(BF16)
    lane = iota((wide, edge), 1)
    pick_t[...] = jnp.where(
        (tall.astype(jnp.int32) == lane // cols)
        & (iota((wide, edge), 0) % cols == lane % cols),
        1.0,
        0.0,
    ).astype(BF16)

    exchange_wait(0)
    reply(1, combine(0))
    exchange_start(1)
    exchange_wait(1)
    spread(1)
    forward_tiles()
    gather_rows()

    sums_start(0, to_row(column_sums(hub_stage), 0))
    set_source(lambda b: hub_stage[b * cols : (b + 1) * cols, :], True)
    transpose_tiles(0, tile_total, True)
    scatter_to_slots(2)
    exchange_start(2)
    scale = 1.0 / jnp.sqrt(to_column(sums_wait(0), 0) / node_total + EPS)
    exchange_wait(2)
    auth_stage[...] = combine(2) * jnp.concatenate([scale] * blocks, axis=0)
    reply(3, auth_stage[...])
    exchange_start(3)
    auth_row = to_row(column_sums(auth_stage), cols)
    exchange_wait(3)
    spread(3)
    forward_tiles()
    gather_rows()
    sums_start(1, to_row(column_sums(hub_stage), 0) + auth_row)
    totals = sums_wait(1)
    hub_scale = 1.0 / jnp.sqrt(to_column(totals, 0) / node_total + EPS)
    auth_scale = 1.0 / jnp.sqrt(to_column(totals, cols) / node_total + EPS)
    for b in range(blocks):
        here = slice(b * cols, (b + 1) * cols)
        hub_out[:, b * edge : (b + 1) * edge] = hub_stage[here, :] * hub_scale
        auth_out[:, b * edge : (b + 1) * edge] = auth_stage[here, :] * auth_scale

    wait_bytes(recv_idx, idx_send_sem)
    for which in range(2):
        wait_bytes(recv_sum.at[which], sum_send_sem.at[which])
    for phase in range(4):
        wait_bytes(recv.at[phase], send_sem.at[phase])


def per_device(edge_tiles, tile_row, tile_slot, tile_count, fetch_list, hub_start):
    devices = lax.axis_size(AXIS)
    tile_total, edge, _ = edge_tiles.shape
    cols, nodes = hub_start.shape
    blocks = nodes // edge
    slots_total = fetch_list.shape[1]
    part = slots_total // devices * cols
    smem = pl.BlockSpec(memory_space=pltpu.SMEM)
    vmem = pl.BlockSpec(memory_space=pltpu.VMEM)
    dma = pltpu.SemaphoreType.DMA
    return pl.pallas_call(
        functools.partial(kernel, devices, nodes * devices),
        out_shape=(jax.ShapeDtypeStruct((cols, nodes), F32),) * 2,
        in_specs=[smem, smem, smem, pl.BlockSpec(memory_space=pl.ANY)] + [vmem] * 4,
        out_specs=(vmem, vmem),
        scratch_shapes=[
            pltpu.VMEM((tile_total, edge, edge), BF16),
            pltpu.VMEM((cols * tile_total, edge), F32),
            pltpu.VMEM((slots_total * cols, edge), F32),
            pltpu.VMEM((slots_total, cols, edge), F32),
            pltpu.VMEM((slots_total, tile_total), BF16),
            pltpu.VMEM((slots_total * cols, edge), BF16),
            pltpu.VMEM((blocks * cols, slots_total * cols), BF16),
        ]
        + [pltpu.VMEM((blocks, 2 * cols, edge), BF16)] * 4
        + [
            pltpu.VMEM((blocks * cols, edge), F32),
            pltpu.VMEM((blocks * cols, edge), F32),
            pltpu.VMEM((4, devices, part, edge), BF16),
            pltpu.VMEM((4, devices, part, edge), BF16),
            pltpu.VMEM((devices, 1, slots_total), jnp.int32),
            pltpu.VMEM((2, 1, edge), F32),
            pltpu.VMEM((2, devices, 1, edge), F32),
            dma((CHUNKS,)),
            dma((4,)),
            dma((4,)),
            dma,
            dma,
            dma((2,)),
            dma((2,)),
        ],
        compiler_params=pltpu.CompilerParams(
            collective_id=0, has_side_effects=True, vmem_limit_bytes=60 << 20
        ),
    )(
        tile_row,
        tile_slot,
        tile_count,
        edge_tiles,
        tile_row.reshape(1, tile_total),
        tile_slot.reshape(1, tile_total),
        fetch_list,
        hub_start,
    )


def solution(mesh):
    placed = (P(AXIS, None, None), P(AXIS), P(AXIS), P(AXIS), P(AXIS, None), P(None, AXIS))
    return jax.shard_map(
        per_device,
        mesh=mesh,
        in_specs=placed,
        out_specs=(P(None, AXIS), P(None, AXIS)),
        check_vma=False,
    )
```

```python
import functools

import jax
import jax.numpy as jnp
import numpy as np
from jax import lax
from jax.experimental import pallas as pl
from jax.experimental.pallas import tpu as pltpu
from jax.sharding import PartitionSpec as P

AXIS = "rows"
EPS = 1e-06
F32 = jnp.float32
BF16 = jnp.bfloat16
CHUNKS = 4
QUADS = 32
TURNS = 8
GRID = (4, 4, 4, 2)
MESH = pl.DeviceIdType.MESH


def dot_nn(lhs, rhs):
    return lax.dot_general(lhs, rhs, (((1,), (0,)), ((), ())), preferred_element_type=F32)


def split_bf16(x):
    high = x.astype(BF16)
    return high, (x - high.astype(F32)).astype(BF16)


def iota(shape, dim):
    return lax.broadcasted_iota(jnp.int32, shape, dim)


def ring_distance(offset):
    return [min(o, size - o) for o, size in zip(offset[:3], GRID)]


def send_order():
    def key(offset):
        away = ring_distance(offset)
        return (-sum(d > 0 for d in away), -sum(away), offset)

    every = list(np.ndindex(*GRID))[1:]
    ordered = []
    for offset in sorted(every, key=key):
        back = tuple((size - o) % size for o, size in zip(offset[:3], GRID)) + offset[3:]
        for each in (offset, back):
            if each not in ordered:
                ordered.append(each)
    return ordered


def kernel(
    devices,
    node_total,
    rows_s,
    slots_s,
    count_s,
    tiles_hbm,
    rows_v,
    slots_v,
    fetch_v,
    hub_v,
    hub_out,
    auth_out,
    tiles,
    turned,
    prod,
    stage,
    fetched,
    onehot_slot,
    pick_t,
    pick,
    src_a,
    src_b,
    src_al,
    src_bl,
    hub_stage,
    auth_stage,
    send,
    recv,
    send_idx,
    recv_idx,
    send_sum,
    recv_sum,
    tile_sem,
    send_sem,
    recv_sem,
    idx_send_sem,
    idx_recv_sem,
    sum_send_sem,
    sum_recv_sem,
):
    tile_total, edge, _ = tiles.shape
    cols = hub_v.shape[0]
    blocks = hub_v.shape[1] // edge
    slots_total = fetch_v.shape[1]
    slots_each = slots_total // devices
    part = slots_each * cols
    me = lax.axis_index(AXIS)
    barrier = pltpu.get_barrier_semaphore()

    order = send_order()
    place = []
    inner = 1
    for size in GRID[::-1]:
        here = lax.rem(me // inner, size)
        place.insert(0, [lax.rem(here + k, size) * inner for k in range(size)])
        inner *= size
    outer_part = [[a + b for b in place[1]] for a in place[0]]
    inner_part = [[a + b for b in place[3]] for a in place[2]]

    def target(offset):
        return outer_part[offset[0]][offset[1]] + inner_part[offset[2]][offset[3]]

    per_chunk = tile_total // CHUNKS
    for q in range(CHUNKS):
        window = pl.ds(q * per_chunk, per_chunk)
        pltpu.make_async_copy(tiles_hbm.at[window], tiles.at[window], tile_sem.at[q]).start()

    for offset in order:
        pl.semaphore_signal(barrier, inc=1, device_id=(target(offset),), device_id_type=MESH)

    zero_block = jnp.zeros((cols, edge), F32)

    def set_source(blocks_f32, with_low):
        for b in range(blocks):
            x = blocks_f32(b)
            up = jnp.concatenate([x, zero_block], axis=0)
            down = jnp.concatenate([zero_block, x], axis=0)
            if with_low:
                src_a[b], src_al[b] = split_bf16(up)
                src_b[b], src_bl[b] = split_bf16(down)
            else:
                src_a[b] = up.astype(BF16)
                src_b[b] = down.astype(BF16)

    def store_quad(t, o):
        prod[pl.ds(t, cols, stride=tile_total), :] = o[:cols, :edge]
        prod[pl.ds(t + 1, cols, stride=tile_total), :] = o[cols : 2 * cols, :edge]
        prod[pl.ds(t + 2, cols, stride=tile_total), :] = o[2 * cols : 3 * cols, edge:]
        prod[pl.ds(t + 3, cols, stride=tile_total), :] = o[3 * cols :, edge:]

    def quad_lhs(a, b, t):
        r = [rows_s[t + q] for q in range(4)]
        return jnp.concatenate(
            [
                jnp.concatenate([a[r[0]], b[r[1]]], axis=1),
                jnp.concatenate([a[r[2]], b[r[3]]], axis=1),
            ],
            axis=0,
        )

    def quad_rhs(ref, t):
        return jnp.concatenate(
            [
                ref[pl.ds(t, 2)].reshape(2 * edge, edge),
                ref[pl.ds(t + 2, 2)].reshape(2 * edge, edge),
            ],
            axis=1,
        )

    def transpose_tiles(first, total, quads, with_low, beside=None):
        def body(i, carry):
            if beside is not None:
                beside(i)
            for u in range(quads):
                t = first + (i * quads + u) * 4
                lhs = quad_lhs(src_a, src_b, t)
                if with_low:
                    lhs = jnp.concatenate([lhs, quad_lhs(src_al, src_bl, t)], axis=0)
                o = dot_nn(lhs, quad_rhs(tiles, t))
                if with_low:
                    o = o[: 4 * cols] + o[4 * cols :]
                store_quad(t, o)
            return carry

        lax.fori_loop(0, total // (4 * quads), body, 0)

    def forward_tiles():
        def body(i, carry):
            for u in range(QUADS):
                t = (i * QUADS + u) * 4
                f = [fetched[slots_s[t + q]] for q in range(4)]
                lhs = jnp.concatenate(
                    [
                        jnp.concatenate([f[0], zero_block, f[2], zero_block], axis=0),
                        jnp.concatenate([zero_block, f[1], zero_block, f[3]], axis=0),
                    ],
                    axis=1,
                ).astype(BF16)
                store_quad(t, dot_nn(lhs, quad_rhs(turned, t)))
            return carry

        lax.fori_loop(0, tile_total // (4 * QUADS), body, 0)

    def turn_tiles():
        def body(i, carry):
            for u in range(TURNS):
                t = i * TURNS + u
                turned[t] = tiles[t].T
            return carry

        lax.fori_loop(0, tile_total // TURNS, body, 0)

    def prod_split(c):
        return split_bf16(prod[c * tile_total : (c + 1) * tile_total, :])

    def scatter_to_slots(phase):
        chooser = onehot_slot[...]
        for c in range(cols):
            high, low = prod_split(c)
            total = dot_nn(chooser, high) + dot_nn(chooser, low)
            stage[pl.ds(c, slots_total, stride=cols), :] = total
        send[phase] = stage[...].astype(BF16).reshape(devices, part, edge)

    def exchange_start(phase):
        for offset in order:
            d = target(offset)
            pltpu.make_async_remote_copy(
                src_ref=send.at[phase, d],
                dst_ref=recv.at[phase, me],
                send_sem=send_sem.at[phase],
                recv_sem=recv_sem.at[phase],
                device_id=(d,),
                device_id_type=MESH,
            ).start()

        recv[phase, me] = send[phase, me]

    def wait_bytes(ref, sem):
        others = ref.at[pl.ds(0, devices - 1)]
        pltpu.make_async_copy(others, others, sem).wait()

    def exchange_wait(phase):
        wait_bytes(recv.at[phase], recv_sem.at[phase])

    def sums_send(which, d):
        pltpu.make_async_remote_copy(
            src_ref=send_sum.at[which],
            dst_ref=recv_sum.at[which, me],
            send_sem=sum_send_sem.at[which],
            recv_sem=sum_recv_sem.at[which],
            device_id=(d,),
            device_id_type=MESH,
        ).start()

    def sums_ready(which, row):
        send_sum[which] = row
        recv_sum[which, me] = row

    def sums_wait(which):
        wait_bytes(recv_sum.at[which], sum_recv_sem.at[which])
        return jnp.sum(recv_sum[which], axis=0)

    def to_row(column, offset):
        spot = iota((cols, edge), 1) == iota((cols, edge), 0) + offset
        return jnp.sum(jnp.where(spot, column, 0.0), axis=0, keepdims=True)

    def to_column(row, offset):
        spot = iota((cols, edge), 1) == iota((cols, edge), 0) + offset
        return jnp.sum(jnp.where(spot, row, 0.0), axis=1, keepdims=True)

    def combine(phase):
        arrived = recv[phase].reshape(slots_total * cols, edge)
        return dot_nn(pick[...], arrived)

    def reply(phase, authority):
        low = authority.astype(BF16)
        low = jnp.concatenate([low, jnp.zeros_like(low)], axis=0)
        answer = dot_nn(pick_t[...], low).astype(BF16)
        send[phase] = answer.reshape(devices, part, edge)

    def gather_rows():
        alive = iota((blocks, tile_total), 1) < count_s[0]
        chooser = jnp.where(
            alive & (rows_v[...] == iota((blocks, tile_total), 0)), 1.0, 0.0
        ).astype(BF16)
        for c in range(cols):
            high, low = prod_split(c)
            total = dot_nn(chooser, high) + dot_nn(chooser, low)
            hub_stage[pl.ds(c, blocks, stride=cols), :] = total

    def column_sums(ref):
        total = jnp.zeros((cols, edge), F32)
        for b in range(blocks):
            x = ref[b * cols : (b + 1) * cols, :]
            total = total + x * x
        return jnp.sum(total, axis=1, keepdims=True)

    def spread(phase):
        arrived = recv[phase].reshape(slots_total * cols, edge)
        fetched[...] = arrived.astype(F32).reshape(slots_total, cols, edge)

    set_source(lambda b: hub_v[:, b * edge : (b + 1) * edge], False)
    alive = iota((slots_total, tile_total), 1) < count_s[0]
    onehot_slot[...] = jnp.where(
        alive & (slots_v[...] == iota((slots_total, tile_total), 0)), 1.0, 0.0
    ).astype(BF16)
    for q in range(CHUNKS):
        window = pl.ds(q * per_chunk, per_chunk)
        pltpu.make_async_copy(tiles_hbm.at[window], tiles.at[window], tile_sem.at[q]).wait()
        transpose_tiles(q * per_chunk, per_chunk, per_chunk // 4, False)
    scatter_to_slots(0)
    index = iota((slots_total, edge), 0)
    weight = jnp.where(index % slots_each == 0, 1.0, 1.0 * blocks)
    packer = jnp.where(index // slots_each == iota((slots_total, edge), 1), weight, 0.0)
    list_row = jnp.broadcast_to(fetch_v[...].astype(F32), (cols, slots_total))
    list_row = dot_nn(list_row.astype(BF16), packer.astype(BF16))[:1]
    send_idx[...] = list_row
    pl.semaphore_wait(barrier, devices - 1)

    for offset in order:
        d = target(offset)
        pltpu.make_async_remote_copy(
            src_ref=send_idx,
            dst_ref=recv_idx.at[me],
            send_sem=idx_send_sem,
            recv_sem=idx_recv_sem,
            device_id=(d,),
            device_id_type=MESH,
        ).start()
    recv_idx[me] = list_row
    exchange_start(0)

    wait_bytes(recv_idx, idx_recv_sem)
    lists = recv_idx[...].reshape(devices, edge)
    pair = jnp.sum(jnp.where(iota((devices, edge), 1) == me, lists, 0.0), axis=1, keepdims=True)
    pair = jnp.broadcast_to(pair, (devices, edge)).astype(jnp.int32)
    columns = [(pair % blocks).astype(F32), (pair // blocks).astype(F32)]
    wide = slots_total * cols
    line = jnp.zeros((cols, wide), F32)
    tall = jnp.zeros((wide, edge), F32)
    for k in range(slots_each):
        j = iota((devices, wide), 1)
        p = iota((devices, wide), 0)
        expand = jnp.where((j // part == p) & ((j // cols) % slots_each == k), 1.0, 0.0)
        line = line + dot_nn(columns[k].T[:cols].astype(BF16), expand.astype(BF16))
        j = iota((wide, devices), 0)
        p = iota((wide, devices), 1)
        expand = jnp.where((j // part == p) & ((j // cols) % slots_each == k), 1.0, 0.0)
        tall = tall + dot_nn(expand.astype(BF16), columns[k].astype(BF16))
    line_blocks = line.astype(jnp.int32)
    same = iota((cols, wide), 1) % cols == iota((cols, wide), 0)
    for b in range(0, blocks, 2):
        pick[b * cols : (b + 2) * cols, :] = jnp.concatenate(
            [jnp.where((line_blocks == b + h) & same, 1.0, 0.0) for h in range(2)], axis=0
        ).astype(BF16)
    lane = iota((wide, edge), 1)
    pick_t[...] = jnp.where(
        (tall.astype(jnp.int32) == lane // cols)
        & (iota((wide, edge), 0) % cols == lane % cols),
        1.0,
        0.0,
    ).astype(BF16)

    exchange_wait(0)
    reply(1, combine(0))
    exchange_start(1)
    turn_tiles()
    exchange_wait(1)
    spread(1)
    forward_tiles()
    gather_rows()

    sums_ready(0, to_row(column_sums(hub_stage), 0))
    set_source(lambda b: hub_stage[b * cols : (b + 1) * cols, :], True)
    steps = tile_total // (4 * QUADS)
    each = devices // steps
    for i in range(1, steps):
        sums_send(0, lax.rem(me + i * each, devices))

    def sums_beside(i):
        for u in range(1, each):
            sums_send(0, lax.rem(me + i * each + u, devices))

    transpose_tiles(0, tile_total, QUADS, True, sums_beside)
    scatter_to_slots(2)
    exchange_start(2)
    scale = 1.0 / jnp.sqrt(to_column(sums_wait(0), 0) / node_total + EPS)
    exchange_wait(2)
    auth_stage[...] = combine(2) * jnp.concatenate([scale] * blocks, axis=0)
    reply(3, auth_stage[...])
    exchange_start(3)
    auth_row = to_row(column_sums(auth_stage), cols)
    exchange_wait(3)
    spread(3)
    forward_tiles()
    gather_rows()
    sums_ready(1, to_row(column_sums(hub_stage), 0) + auth_row)
    for offset in order:
        sums_send(1, target(offset))
    totals = sums_wait(1)
    hub_scale = 1.0 / jnp.sqrt(to_column(totals, 0) / node_total + EPS)
    auth_scale = 1.0 / jnp.sqrt(to_column(totals, cols) / node_total + EPS)
    for b in range(blocks):
        here = slice(b * cols, (b + 1) * cols)
        hub_out[:, b * edge : (b + 1) * edge] = hub_stage[here, :] * hub_scale
        auth_out[:, b * edge : (b + 1) * edge] = auth_stage[here, :] * auth_scale

    wait_bytes(recv_idx, idx_send_sem)
    for which in range(2):
        wait_bytes(recv_sum.at[which], sum_send_sem.at[which])
    for phase in range(4):
        wait_bytes(recv.at[phase], send_sem.at[phase])


def finish_kernel(hub_in, auth_in, hub_out, auth_out):
    hub_out[...] = hub_in[...]
    auth_out[...] = auth_in[...]


def finish(hub, authority):
    vmem = pl.BlockSpec(memory_space=pltpu.VMEM)
    return pl.pallas_call(
        finish_kernel,
        out_shape=(jax.ShapeDtypeStruct(hub.shape, F32),) * 2,
        in_specs=[vmem] * 2,
        out_specs=(vmem, vmem),
    )(hub, authority)


def per_device(edge_tiles, tile_row, tile_slot, tile_count, fetch_list, hub_start):
    devices = lax.axis_size(AXIS)
    tile_total, edge, _ = edge_tiles.shape
    cols, nodes = hub_start.shape
    blocks = nodes // edge
    slots_total = fetch_list.shape[1]
    part = slots_total // devices * cols
    smem = pl.BlockSpec(memory_space=pltpu.SMEM)
    vmem = pl.BlockSpec(memory_space=pltpu.VMEM)
    dma = pltpu.SemaphoreType.DMA
    results = pl.pallas_call(
        functools.partial(kernel, devices, nodes * devices),
        out_shape=(jax.ShapeDtypeStruct((cols, nodes), F32),) * 2,
        in_specs=[smem, smem, smem, pl.BlockSpec(memory_space=pl.ANY)] + [vmem] * 4,
        out_specs=(vmem, vmem),
        scratch_shapes=[
            pltpu.VMEM((tile_total, edge, edge), BF16),
            pltpu.VMEM((tile_total, edge, edge), BF16),
            pltpu.VMEM((cols * tile_total, edge), F32),
            pltpu.VMEM((slots_total * cols, edge), F32),
            pltpu.VMEM((slots_total, cols, edge), F32),
            pltpu.VMEM((slots_total, tile_total), BF16),
            pltpu.VMEM((slots_total * cols, edge), BF16),
            pltpu.VMEM((blocks * cols, slots_total * cols), BF16),
        ]
        + [pltpu.VMEM((blocks, 2 * cols, edge), BF16)] * 4
        + [
            pltpu.VMEM((blocks * cols, edge), F32),
            pltpu.VMEM((blocks * cols, edge), F32),
            pltpu.VMEM((4, devices, part, edge), BF16),
            pltpu.VMEM((4, devices, part, edge), BF16),
            pltpu.VMEM((1, edge), F32),
            pltpu.VMEM((devices, 1, edge), F32),
            pltpu.VMEM((2, 1, edge), F32),
            pltpu.VMEM((2, devices, 1, edge), F32),
            dma((CHUNKS,)),
            dma((4,)),
            dma((4,)),
            dma,
            dma,
            dma((2,)),
            dma((2,)),
        ],
        compiler_params=pltpu.CompilerParams(
            collective_id=0, has_side_effects=True, vmem_limit_bytes=60 << 20
        ),
    )(
        tile_row,
        tile_slot,
        tile_count,
        edge_tiles,
        tile_row.reshape(1, tile_total),
        tile_slot.reshape(1, tile_total),
        fetch_list,
        hub_start,
    )
    return finish(*results)


def solution(mesh):
    placed = (P(AXIS, None, None), P(AXIS), P(AXIS), P(AXIS), P(AXIS, None), P(None, AXIS))
    return jax.shard_map(
        per_device,
        mesh=mesh,
        in_specs=placed,
        out_specs=(P(None, AXIS), P(None, AXIS)),
        check_vma=False,
    )
```

```python
import functools

import jax
import jax.numpy as jnp
import numpy as np
from jax import lax
from jax.experimental import pallas as pl
from jax.experimental.pallas import tpu as pltpu
from jax.sharding import PartitionSpec as P

AXIS = "rows"
EPS = 1e-06
F32 = jnp.float32
BF16 = jnp.bfloat16
CHUNKS = 4
QUADS = 32
TURNS = 8
HALVES = 2
GRID = (4, 4, 4, 2)
MESH = pl.DeviceIdType.MESH


def dot_nn(lhs, rhs):
    return lax.dot_general(lhs, rhs, (((1,), (0,)), ((), ())), preferred_element_type=F32)


def split_bf16(x):
    high = x.astype(BF16)
    return high, (x - high.astype(F32)).astype(BF16)


def iota(shape, dim):
    return lax.broadcasted_iota(jnp.int32, shape, dim)


def ring_distance(offset):
    return [min(o, size - o) for o, size in zip(offset[:3], GRID)]


def send_order():
    def key(offset):
        away = ring_distance(offset)
        return (-sum(d > 0 for d in away), -sum(away), offset)

    every = list(np.ndindex(*GRID))[1:]
    ordered = []
    for offset in sorted(every, key=key):
        back = tuple((size - o) % size for o, size in zip(offset[:3], GRID)) + offset[3:]
        for each in (offset, back):
            if each not in ordered:
                ordered.append(each)
    return ordered


def kernel(
    devices,
    node_total,
    rows_s,
    slots_s,
    count_s,
    tiles_hbm,
    rows_v,
    slots_v,
    fetch_v,
    hub_v,
    hub_out,
    auth_out,
    tiles,
    turned,
    prod,
    stage,
    fetched,
    onehot_slot,
    pick_t,
    pick,
    src_a,
    src_b,
    src_al,
    src_bl,
    hub_stage,
    auth_stage,
    send,
    recv,
    send_idx,
    recv_idx,
    send_sum,
    recv_sum,
    tile_sem,
    send_sem,
    recv_sem,
    idx_send_sem,
    idx_recv_sem,
    sum_send_sem,
    sum_recv_sem,
):
    tile_total, edge, _ = tiles.shape
    cols = hub_v.shape[0]
    blocks = hub_v.shape[1] // edge
    slots_total = fetch_v.shape[1]
    slots_each = slots_total // devices
    half = cols // HALVES
    part = slots_each * half
    wide = slots_total * half
    me = lax.axis_index(AXIS)
    barrier = pltpu.get_barrier_semaphore()

    order = send_order()
    place = []
    inner = 1
    for size in GRID[::-1]:
        here = lax.rem(me // inner, size)
        place.insert(0, [lax.rem(here + k, size) * inner for k in range(size)])
        inner *= size
    outer_part = [[a + b for b in place[1]] for a in place[0]]
    inner_part = [[a + b for b in place[3]] for a in place[2]]

    def target(offset):
        return outer_part[offset[0]][offset[1]] + inner_part[offset[2]][offset[3]]

    per_chunk = tile_total // CHUNKS
    for q in range(CHUNKS):
        window = pl.ds(q * per_chunk, per_chunk)
        pltpu.make_async_copy(tiles_hbm.at[window], tiles.at[window], tile_sem.at[q]).start()

    for offset in order:
        pl.semaphore_signal(barrier, inc=1, device_id=(target(offset),), device_id_type=MESH)

    zero_block = jnp.zeros((cols, edge), F32)

    def set_source(blocks_f32, with_low):
        for b in range(blocks):
            x = blocks_f32(b)
            up = jnp.concatenate([x, zero_block], axis=0)
            down = jnp.concatenate([zero_block, x], axis=0)
            if with_low:
                src_a[b], src_al[b] = split_bf16(up)
                src_b[b], src_bl[b] = split_bf16(down)
            else:
                src_a[b] = up.astype(BF16)
                src_b[b] = down.astype(BF16)

    def store_quad(t, o):
        prod[pl.ds(t, cols, stride=tile_total), :] = o[:cols, :edge]
        prod[pl.ds(t + 1, cols, stride=tile_total), :] = o[cols : 2 * cols, :edge]
        prod[pl.ds(t + 2, cols, stride=tile_total), :] = o[2 * cols : 3 * cols, edge:]
        prod[pl.ds(t + 3, cols, stride=tile_total), :] = o[3 * cols :, edge:]

    def quad_lhs(a, b, t):
        r = [rows_s[t + q] for q in range(4)]
        return jnp.concatenate(
            [
                jnp.concatenate([a[r[0]], b[r[1]]], axis=1),
                jnp.concatenate([a[r[2]], b[r[3]]], axis=1),
            ],
            axis=0,
        )

    def quad_rhs(ref, t):
        return jnp.concatenate(
            [
                ref[pl.ds(t, 2)].reshape(2 * edge, edge),
                ref[pl.ds(t + 2, 2)].reshape(2 * edge, edge),
            ],
            axis=1,
        )

    def transpose_tiles(first, total, quads, with_low, beside=None):
        def body(i, carry):
            if beside is not None:
                beside(i)
            for u in range(quads):
                t = first + (i * quads + u) * 4
                lhs = quad_lhs(src_a, src_b, t)
                if with_low:
                    lhs = jnp.concatenate([lhs, quad_lhs(src_al, src_bl, t)], axis=0)
                o = dot_nn(lhs, quad_rhs(tiles, t))
                if with_low:
                    o = o[: 4 * cols] + o[4 * cols :]
                store_quad(t, o)
            return carry

        lax.fori_loop(0, total // (4 * quads), body, 0)

    def forward_tiles():
        def body(i, carry):
            for u in range(QUADS):
                t = (i * QUADS + u) * 4
                f = [fetched[slots_s[t + q]] for q in range(4)]
                lhs = jnp.concatenate(
                    [
                        jnp.concatenate([f[0], zero_block, f[2], zero_block], axis=0),
                        jnp.concatenate([zero_block, f[1], zero_block, f[3]], axis=0),
                    ],
                    axis=1,
                ).astype(BF16)
                store_quad(t, dot_nn(lhs, quad_rhs(turned, t)))
            return carry

        lax.fori_loop(0, tile_total // (4 * QUADS), body, 0)

    def turn_tiles():
        def body(i, carry):
            for u in range(TURNS):
                t = i * TURNS + u
                turned[t] = tiles[t].T
            return carry

        lax.fori_loop(0, tile_total // TURNS, body, 0)

    def prod_split(c):
        return split_bf16(prod[c * tile_total : (c + 1) * tile_total, :])

    def scatter_to_slots(phase, h):
        chooser = onehot_slot[...]
        for c in range(half):
            high, low = prod_split(h * half + c)
            total = dot_nn(chooser, high) + dot_nn(chooser, low)
            stage[h, pl.ds(c, slots_total, stride=half), :] = total
        send[phase, h] = stage[h].astype(BF16).reshape(devices, part, edge)

    def exchange_start(phase, h):
        for offset in order:
            d = target(offset)
            pltpu.make_async_remote_copy(
                src_ref=send.at[phase, h, d],
                dst_ref=recv.at[phase, h, me],
                send_sem=send_sem.at[phase, h],
                recv_sem=recv_sem.at[phase, h],
                device_id=(d,),
                device_id_type=MESH,
            ).start()
        recv[phase, h, me] = send[phase, h, me]

    def wait_bytes(ref, sem):
        others = ref.at[pl.ds(0, devices - 1)]
        pltpu.make_async_copy(others, others, sem).wait()

    def exchange_wait(phase, h):
        wait_bytes(recv.at[phase, h], recv_sem.at[phase, h])

    def sums_send(which, d):
        pltpu.make_async_remote_copy(
            src_ref=send_sum.at[which],
            dst_ref=recv_sum.at[which, me],
            send_sem=sum_send_sem.at[which],
            recv_sem=sum_recv_sem.at[which],
            device_id=(d,),
            device_id_type=MESH,
        ).start()

    def sums_ready(which, row):
        send_sum[which] = row
        recv_sum[which, me] = row

    def sums_wait(which):
        wait_bytes(recv_sum.at[which], sum_recv_sem.at[which])
        return jnp.sum(recv_sum[which], axis=0)

    def to_row(column, offset, period):
        spot = iota((cols, edge), 1) == iota((cols, edge), 0) % period + offset
        return jnp.sum(jnp.where(spot, column, 0.0), axis=0, keepdims=True)

    def to_column(row, offset, period):
        spot = iota((cols, edge), 1) == iota((cols, edge), 0) % period + offset
        return jnp.sum(jnp.where(spot, row, 0.0), axis=1, keepdims=True)

    def inverse_norm(row, offset, period):
        return 1.0 / jnp.sqrt(to_column(row, offset, period) / node_total + EPS)

    def combine(phase, h):
        return dot_nn(pick[...], recv[phase, h].reshape(wide, edge))

    def reply(phase, h, authority):
        low = authority.astype(BF16)
        low = jnp.concatenate([low, jnp.zeros((edge - blocks * half, edge), BF16)], axis=0)
        answer = dot_nn(pick_t[...], low).astype(BF16)
        send[phase, h] = answer.reshape(devices, part, edge)

    def gather_rows():
        alive = iota((blocks, tile_total), 1) < count_s[0]
        chooser = jnp.where(
            alive & (rows_v[...] == iota((blocks, tile_total), 0)), 1.0, 0.0
        ).astype(BF16)
        for c in range(cols):
            high, low = prod_split(c)
            total = dot_nn(chooser, high) + dot_nn(chooser, low)
            hub_stage[pl.ds(c, blocks, stride=cols), :] = total

    def column_sums(ref):
        total = jnp.zeros((cols, edge), F32)
        for g in range(ref.shape[0] // cols):
            x = ref[g * cols : (g + 1) * cols, :]
            total = total + x * x
        return jnp.sum(total, axis=1, keepdims=True)

    def spread(phase, h):
        arrived = recv[phase, h].reshape(wide, edge).astype(F32)
        fetched[:, h * half : (h + 1) * half, :] = arrived.reshape(slots_total, half, edge)

    set_source(lambda b: hub_v[:, b * edge : (b + 1) * edge], False)
    alive = iota((slots_total, tile_total), 1) < count_s[0]
    onehot_slot[...] = jnp.where(
        alive & (slots_v[...] == iota((slots_total, tile_total), 0)), 1.0, 0.0
    ).astype(BF16)
    for q in range(CHUNKS):
        window = pl.ds(q * per_chunk, per_chunk)
        pltpu.make_async_copy(tiles_hbm.at[window], tiles.at[window], tile_sem.at[q]).wait()
        transpose_tiles(q * per_chunk, per_chunk, per_chunk // 4, False)
    for h in range(HALVES):
        scatter_to_slots(0, h)
    index = iota((slots_total, edge), 0)
    weight = jnp.where(index % slots_each == 0, 1.0, 1.0 * blocks)
    packer = jnp.where(index // slots_each == iota((slots_total, edge), 1), weight, 0.0)
    list_row = jnp.broadcast_to(fetch_v[...].astype(F32), (cols, slots_total))
    list_row = dot_nn(list_row.astype(BF16), packer.astype(BF16))[:1]
    send_idx[...] = list_row
    pl.semaphore_wait(barrier, devices - 1)

    for offset in order:
        d = target(offset)
        pltpu.make_async_remote_copy(
            src_ref=send_idx,
            dst_ref=recv_idx.at[me],
            send_sem=idx_send_sem,
            recv_sem=idx_recv_sem,
            device_id=(d,),
            device_id_type=MESH,
        ).start()
    recv_idx[me] = list_row
    for h in range(HALVES):
        exchange_start(0, h)

    wait_bytes(recv_idx, idx_recv_sem)
    lists = recv_idx[...].reshape(devices, edge)
    pair = jnp.sum(jnp.where(iota((devices, edge), 1) == me, lists, 0.0), axis=1, keepdims=True)
    pair = jnp.broadcast_to(pair, (devices, edge)).astype(jnp.int32)
    columns = [(pair % blocks).astype(F32), (pair // blocks).astype(F32)]
    line = jnp.zeros((cols, wide), F32)
    tall = jnp.zeros((wide, edge), F32)
    for k in range(slots_each):
        j = iota((devices, wide), 1)
        p = iota((devices, wide), 0)
        expand = jnp.where((j // part == p) & ((j // half) % slots_each == k), 1.0, 0.0)
        line = line + dot_nn(columns[k].T[:cols].astype(BF16), expand.astype(BF16))
        j = iota((wide, devices), 0)
        p = iota((wide, devices), 1)
        expand = jnp.where((j // part == p) & ((j // half) % slots_each == k), 1.0, 0.0)
        tall = tall + dot_nn(expand.astype(BF16), columns[k].astype(BF16))
    line_blocks = line.astype(jnp.int32)
    row = iota((cols, wide), 0)
    same = iota((cols, wide), 1) % half == row % half
    for b in range(0, blocks, 4):
        pick[b * half : (b + 4) * half, :] = jnp.concatenate(
            [
                jnp.where((line_blocks == b + g + row // half) & same, 1.0, 0.0)
                for g in range(0, 4, cols // half)
            ],
            axis=0,
        ).astype(BF16)
    lane = iota((wide, edge), 1)
    pick_t[...] = jnp.where(
        (tall.astype(jnp.int32) == lane // half)
        & (iota((wide, edge), 0) % half == lane % half),
        1.0,
        0.0,
    ).astype(BF16)

    for h in range(HALVES):
        exchange_wait(0, h)
        reply(1, h, combine(0, h))
        exchange_start(1, h)
    turn_tiles()
    for h in range(HALVES):
        exchange_wait(1, h)
        spread(1, h)
    forward_tiles()
    gather_rows()

    sums_ready(0, to_row(column_sums(hub_stage), 0, cols))
    set_source(lambda b: hub_stage[b * cols : (b + 1) * cols, :], True)
    steps = tile_total // (4 * QUADS)
    each = devices // steps
    for i in range(1, steps):
        sums_send(0, lax.rem(me + i * each, devices))

    def sums_beside(i):
        for u in range(1, each):
            sums_send(0, lax.rem(me + i * each + u, devices))

    transpose_tiles(0, tile_total, QUADS, True, sums_beside)
    for h in range(HALVES):
        scatter_to_slots(2, h)
        exchange_start(2, h)
    totals = sums_wait(0)
    auth_row = jnp.zeros((1, edge), F32)
    for h in range(HALVES):
        scale = inverse_norm(totals, h * half, half)
        exchange_wait(2, h)
        auth_stage[h] = combine(2, h) * jnp.concatenate([scale] * (blocks * half // cols), axis=0)
        reply(3, h, auth_stage[h])
        exchange_start(3, h)
        auth_row += to_row(column_sums(auth_stage.at[h]), cols + h * half, half)
    for h in range(HALVES):
        exchange_wait(3, h)
        spread(3, h)
    forward_tiles()
    gather_rows()
    sums_ready(1, to_row(column_sums(hub_stage), 0, cols) + auth_row)
    for offset in order:
        sums_send(1, target(offset))
    totals = sums_wait(1)
    hub_scale = inverse_norm(totals, 0, cols)
    for b in range(blocks):
        hub_out[:, b * edge : (b + 1) * edge] = hub_stage[b * cols : (b + 1) * cols, :] * hub_scale
    for h in range(HALVES):
        auth_scale = inverse_norm(totals, cols + h * half, half)
        for g in range(blocks * half // cols):
            both = auth_stage[h, g * cols : (g + 1) * cols, :] * auth_scale
            for q in range(cols // half):
                b = g * (cols // half) + q
                auth_out[h * half : (h + 1) * half, b * edge : (b + 1) * edge] = both[
                    q * half : (q + 1) * half
                ]

    wait_bytes(recv_idx, idx_send_sem)
    for which in range(2):
        wait_bytes(recv_sum.at[which], sum_send_sem.at[which])
    for phase in range(4):
        for h in range(HALVES):
            wait_bytes(recv.at[phase, h], send_sem.at[phase, h])


def finish_kernel(hub_in, auth_in, hub_out, auth_out):
    hub_out[...] = hub_in[...]
    auth_out[...] = auth_in[...]


def finish(hub, authority):
    vmem = pl.BlockSpec(memory_space=pltpu.VMEM)
    return pl.pallas_call(
        finish_kernel,
        out_shape=(jax.ShapeDtypeStruct(hub.shape, F32),) * 2,
        in_specs=[vmem] * 2,
        out_specs=(vmem, vmem),
    )(hub, authority)


def per_device(edge_tiles, tile_row, tile_slot, tile_count, fetch_list, hub_start):
    devices = lax.axis_size(AXIS)
    tile_total, edge, _ = edge_tiles.shape
    cols, nodes = hub_start.shape
    blocks = nodes // edge
    slots_total = fetch_list.shape[1]
    half = cols // HALVES
    part = slots_total // devices * half
    wide = slots_total * half
    smem = pl.BlockSpec(memory_space=pltpu.SMEM)
    vmem = pl.BlockSpec(memory_space=pltpu.VMEM)
    dma = pltpu.SemaphoreType.DMA
    results = pl.pallas_call(
        functools.partial(kernel, devices, nodes * devices),
        out_shape=(jax.ShapeDtypeStruct((cols, nodes), F32),) * 2,
        in_specs=[smem, smem, smem, pl.BlockSpec(memory_space=pl.ANY)] + [vmem] * 4,
        out_specs=(vmem, vmem),
        scratch_shapes=[
            pltpu.VMEM((tile_total, edge, edge), BF16),
            pltpu.VMEM((tile_total, edge, edge), BF16),
            pltpu.VMEM((cols * tile_total, edge), F32),
            pltpu.VMEM((HALVES, wide, edge), F32),
            pltpu.VMEM((slots_total, cols, edge), F32),
            pltpu.VMEM((slots_total, tile_total), BF16),
            pltpu.VMEM((wide, edge), BF16),
            pltpu.VMEM((blocks * half, wide), BF16),
        ]
        + [pltpu.VMEM((blocks, 2 * cols, edge), BF16)] * 4
        + [
            pltpu.VMEM((blocks * cols, edge), F32),
            pltpu.VMEM((HALVES, blocks * half, edge), F32),
            pltpu.VMEM((4, HALVES, devices, part, edge), BF16),
            pltpu.VMEM((4, HALVES, devices, part, edge), BF16),
            pltpu.VMEM((1, edge), F32),
            pltpu.VMEM((devices, 1, edge), F32),
            pltpu.VMEM((2, 1, edge), F32),
            pltpu.VMEM((2, devices, 1, edge), F32),
            dma((CHUNKS,)),
            dma((4, HALVES)),
            dma((4, HALVES)),
            dma,
            dma,
            dma((2,)),
            dma((2,)),
        ],
        compiler_params=pltpu.CompilerParams(
            collective_id=0, has_side_effects=True, vmem_limit_bytes=60 << 20
        ),
    )(
        tile_row,
        tile_slot,
        tile_count,
        edge_tiles,
        tile_row.reshape(1, tile_total),
        tile_slot.reshape(1, tile_total),
        fetch_list,
        hub_start,
    )
    return finish(*results)


def solution(mesh):
    placed = (P(AXIS, None, None), P(AXIS), P(AXIS), P(AXIS), P(AXIS, None), P(None, AXIS))
    return jax.shard_map(
        per_device,
        mesh=mesh,
        in_specs=placed,
        out_specs=(P(None, AXIS), P(None, AXIS)),
        check_vma=False,
    )
```

```python
import functools

import jax
import jax.numpy as jnp
import numpy as np
from jax import lax
from jax.experimental import pallas as pl
from jax.experimental.pallas import tpu as pltpu
from jax.sharding import PartitionSpec as P

AXIS = "rows"
EPS = 1e-06
F32 = jnp.float32
BF16 = jnp.bfloat16
CHUNKS = 4
QUADS = 64
TURNS = 8
HALVES = 4
GRID = (4, 4, 4, 2)
MESH = pl.DeviceIdType.MESH


def dot_nn(lhs, rhs):
    return lax.dot_general(lhs, rhs, (((1,), (0,)), ((), ())), preferred_element_type=F32)


def split_bf16(x):
    high = x.astype(BF16)
    return high, (x - high.astype(F32)).astype(BF16)


def iota(shape, dim):
    return lax.broadcasted_iota(jnp.int32, shape, dim)


def ring_distance(offset):
    return [min(o, size - o) for o, size in zip(offset[:3], GRID)]


def send_order():
    def key(offset):
        away = ring_distance(offset)
        return (-sum(d > 0 for d in away), -sum(away), offset)

    every = list(np.ndindex(*GRID))[1:]
    ordered = []
    for offset in sorted(every, key=key):
        back = tuple((size - o) % size for o, size in zip(offset[:3], GRID)) + offset[3:]
        for each in (offset, back):
            if each not in ordered:
                ordered.append(each)
    return ordered


def kernel(
    devices,
    node_total,
    rows_s,
    slots_s,
    count_s,
    tiles_hbm,
    rows_v,
    slots_v,
    fetch_v,
    hub_v,
    hub_out,
    auth_out,
    tiles,
    turned,
    prod,
    stage,
    fetched,
    onehot_slot,
    pick_t,
    pick,
    src_a,
    src_b,
    src_al,
    src_bl,
    hub_stage,
    auth_stage,
    send,
    recv,
    send_idx,
    recv_idx,
    send_sum,
    recv_sum,
    tile_sem,
    send_sem,
    recv_sem,
    idx_send_sem,
    idx_recv_sem,
    sum_send_sem,
    sum_recv_sem,
):
    tile_total, edge, _ = tiles.shape
    cols = hub_v.shape[0]
    blocks = hub_v.shape[1] // edge
    slots_total = fetch_v.shape[1]
    slots_each = slots_total // devices
    half = cols // HALVES
    part = slots_each * half
    wide = slots_total * half
    me = lax.axis_index(AXIS)
    barrier = pltpu.get_barrier_semaphore()

    order = send_order()
    place = []
    inner = 1
    for size in GRID[::-1]:
        here = lax.rem(me // inner, size)
        place.insert(0, [lax.rem(here + k, size) * inner for k in range(size)])
        inner *= size
    outer_part = [[a + b for b in place[1]] for a in place[0]]
    inner_part = [[a + b for b in place[3]] for a in place[2]]

    def target(offset):
        return outer_part[offset[0]][offset[1]] + inner_part[offset[2]][offset[3]]

    per_chunk = tile_total // CHUNKS
    for q in range(CHUNKS):
        window = pl.ds(q * per_chunk, per_chunk)
        pltpu.make_async_copy(tiles_hbm.at[window], tiles.at[window], tile_sem.at[q]).start()

    for offset in order:
        pl.semaphore_signal(barrier, inc=1, device_id=(target(offset),), device_id_type=MESH)

    zero_block = jnp.zeros((cols, edge), F32)

    def set_source(blocks_f32, with_low):
        for b in range(blocks):
            x = blocks_f32(b)
            up = jnp.concatenate([x, zero_block], axis=0)
            down = jnp.concatenate([zero_block, x], axis=0)
            if with_low:
                src_a[b], src_al[b] = split_bf16(up)
                src_b[b], src_bl[b] = split_bf16(down)
            else:
                src_a[b] = up.astype(BF16)
                src_b[b] = down.astype(BF16)

    def store_quad(t, o):
        prod[pl.ds(t, cols, stride=tile_total), :] = o[:cols, :edge]
        prod[pl.ds(t + 1, cols, stride=tile_total), :] = o[cols : 2 * cols, :edge]
        prod[pl.ds(t + 2, cols, stride=tile_total), :] = o[2 * cols : 3 * cols, edge:]
        prod[pl.ds(t + 3, cols, stride=tile_total), :] = o[3 * cols :, edge:]

    def quad_lhs(a, b, t):
        r = [rows_s[t + q] for q in range(4)]
        return jnp.concatenate(
            [
                jnp.concatenate([a[r[0]], b[r[1]]], axis=1),
                jnp.concatenate([a[r[2]], b[r[3]]], axis=1),
            ],
            axis=0,
        )

    def quad_rhs(ref, t):
        return jnp.concatenate(
            [
                ref[pl.ds(t, 2)].reshape(2 * edge, edge),
                ref[pl.ds(t + 2, 2)].reshape(2 * edge, edge),
            ],
            axis=1,
        )

    def transpose_tiles(first, total, quads, with_low, beside=None):
        def body(i, carry):
            if beside is not None:
                beside(i)
            for u in range(quads):
                t = first + (i * quads + u) * 4
                lhs = quad_lhs(src_a, src_b, t)
                if with_low:
                    lhs = jnp.concatenate([lhs, quad_lhs(src_al, src_bl, t)], axis=0)
                o = dot_nn(lhs, quad_rhs(tiles, t))
                if with_low:
                    o = o[: 4 * cols] + o[4 * cols :]
                store_quad(t, o)
            return carry

        lax.fori_loop(0, total // (4 * quads), body, 0)

    def forward_tiles():
        def body(i, carry):
            for u in range(QUADS):
                t = (i * QUADS + u) * 4
                f = [fetched[slots_s[t + q]] for q in range(4)]
                lhs = jnp.concatenate(
                    [
                        jnp.concatenate([f[0], zero_block, f[2], zero_block], axis=0),
                        jnp.concatenate([zero_block, f[1], zero_block, f[3]], axis=0),
                    ],
                    axis=1,
                ).astype(BF16)
                store_quad(t, dot_nn(lhs, quad_rhs(turned, t)))
            return carry

        lax.fori_loop(0, tile_total // (4 * QUADS), body, 0)

    def turn_tiles():
        def body(i, carry):
            for u in range(TURNS):
                t = i * TURNS + u
                turned[t] = tiles[t].T
            return carry

        lax.fori_loop(0, tile_total // TURNS, body, 0)

    def prod_split(c):
        return split_bf16(prod[c * tile_total : (c + 1) * tile_total, :])

    def scatter_to_slots(phase, h):
        chooser = onehot_slot[...]
        for c in range(half):
            high, low = prod_split(h * half + c)
            total = dot_nn(chooser, high) + dot_nn(chooser, low)
            stage[h, pl.ds(c, slots_total, stride=half), :] = total
        send[phase, h] = stage[h].astype(BF16).reshape(devices, part, edge)

    def exchange_start(phase, h):
        for offset in order:
            d = target(offset)
            pltpu.make_async_remote_copy(
                src_ref=send.at[phase, h, d],
                dst_ref=recv.at[phase, h, me],
                send_sem=send_sem.at[phase, h],
                recv_sem=recv_sem.at[phase, h],
                device_id=(d,),
                device_id_type=MESH,
            ).start()
        recv[phase, h, me] = send[phase, h, me]

    def wait_bytes(ref, sem):
        others = ref.at[pl.ds(0, devices - 1)]
        pltpu.make_async_copy(others, others, sem).wait()

    def exchange_wait(phase, h):
        wait_bytes(recv.at[phase, h], recv_sem.at[phase, h])

    def sums_send(which, d):
        pltpu.make_async_remote_copy(
            src_ref=send_sum.at[which],
            dst_ref=recv_sum.at[which, me],
            send_sem=sum_send_sem.at[which],
            recv_sem=sum_recv_sem.at[which],
            device_id=(d,),
            device_id_type=MESH,
        ).start()

    def sums_ready(which, row):
        send_sum[which] = row
        recv_sum[which, me] = row

    def sums_wait(which):
        wait_bytes(recv_sum.at[which], sum_recv_sem.at[which])
        return jnp.sum(recv_sum[which], axis=0)

    def to_row(column, offset, period):
        spot = iota((cols, edge), 1) == iota((cols, edge), 0) % period + offset
        return jnp.sum(jnp.where(spot, column, 0.0), axis=0, keepdims=True)

    def to_column(row, offset, period):
        spot = iota((cols, edge), 1) == iota((cols, edge), 0) % period + offset
        return jnp.sum(jnp.where(spot, row, 0.0), axis=1, keepdims=True)

    def inverse_norm(row, offset, period):
        return 1.0 / jnp.sqrt(to_column(row, offset, period) / node_total + EPS)

    def combine(phase, h):
        return dot_nn(pick[...], recv[phase, h].reshape(wide, edge))

    def reply(phase, h, authority):
        low = authority.astype(BF16)
        low = jnp.concatenate([low, jnp.zeros((edge - blocks * half, edge), BF16)], axis=0)
        answer = dot_nn(pick_t[...], low).astype(BF16)
        send[phase, h] = answer.reshape(devices, part, edge)

    def gather_rows():
        alive = iota((blocks, tile_total), 1) < count_s[0]
        chooser = jnp.where(
            alive & (rows_v[...] == iota((blocks, tile_total), 0)), 1.0, 0.0
        ).astype(BF16)
        for c in range(cols):
            high, low = prod_split(c)
            total = dot_nn(chooser, high) + dot_nn(chooser, low)
            hub_stage[pl.ds(c, blocks, stride=cols), :] = total

    def column_sums(ref):
        total = jnp.zeros((cols, edge), F32)
        for g in range(ref.shape[0] // cols):
            x = ref[g * cols : (g + 1) * cols, :]
            total = total + x * x
        return jnp.sum(total, axis=1, keepdims=True)

    def spread(phase, h):
        arrived = recv[phase, h].reshape(wide, edge).astype(F32)
        fetched[:, h * half : (h + 1) * half, :] = arrived.reshape(slots_total, half, edge)

    set_source(lambda b: hub_v[:, b * edge : (b + 1) * edge], False)
    alive = iota((slots_total, tile_total), 1) < count_s[0]
    onehot_slot[...] = jnp.where(
        alive & (slots_v[...] == iota((slots_total, tile_total), 0)), 1.0, 0.0
    ).astype(BF16)
    for q in range(CHUNKS):
        window = pl.ds(q * per_chunk, per_chunk)
        pltpu.make_async_copy(tiles_hbm.at[window], tiles.at[window], tile_sem.at[q]).wait()
        transpose_tiles(q * per_chunk, per_chunk, per_chunk // 4, False)
    for h in range(HALVES):
        scatter_to_slots(0, h)
    index = iota((slots_total, edge), 0)
    weight = jnp.where(index % slots_each == 0, 1.0, 1.0 * blocks)
    packer = jnp.where(index // slots_each == iota((slots_total, edge), 1), weight, 0.0)
    list_row = jnp.broadcast_to(fetch_v[...].astype(F32), (cols, slots_total))
    list_row = dot_nn(list_row.astype(BF16), packer.astype(BF16))[:1]
    send_idx[...] = list_row
    pl.semaphore_wait(barrier, devices - 1)

    for offset in order:
        d = target(offset)
        pltpu.make_async_remote_copy(
            src_ref=send_idx,
            dst_ref=recv_idx.at[me],
            send_sem=idx_send_sem,
            recv_sem=idx_recv_sem,
            device_id=(d,),
            device_id_type=MESH,
        ).start()
    recv_idx[me] = list_row
    for h in range(HALVES):
        exchange_start(0, h)

    wait_bytes(recv_idx, idx_recv_sem)
    lists = recv_idx[...].reshape(devices, edge)
    pair = jnp.sum(jnp.where(iota((devices, edge), 1) == me, lists, 0.0), axis=1, keepdims=True)
    pair = jnp.broadcast_to(pair, (devices, edge)).astype(jnp.int32)
    columns = [(pair % blocks).astype(F32), (pair // blocks).astype(F32)]
    line = jnp.zeros((cols, wide), F32)
    tall = jnp.zeros((wide, edge), F32)
    for k in range(slots_each):
        j = iota((devices, wide), 1)
        p = iota((devices, wide), 0)
        expand = jnp.where((j // part == p) & ((j // half) % slots_each == k), 1.0, 0.0)
        line = line + dot_nn(columns[k].T[:cols].astype(BF16), expand.astype(BF16))
        j = iota((wide, devices), 0)
        p = iota((wide, devices), 1)
        expand = jnp.where((j // part == p) & ((j // half) % slots_each == k), 1.0, 0.0)
        tall = tall + dot_nn(expand.astype(BF16), columns[k].astype(BF16))
    line_blocks = line.astype(jnp.int32)
    row = iota((cols, wide), 0)
    same = iota((cols, wide), 1) % half == row % half
    for b in range(0, blocks, 4):
        pick[b * half : (b + 4) * half, :] = jnp.concatenate(
            [
                jnp.where((line_blocks == b + g + row // half) & same, 1.0, 0.0)
                for g in range(0, 4, cols // half)
            ],
            axis=0,
        ).astype(BF16)
    lane = iota((wide, edge), 1)
    pick_t[...] = jnp.where(
        (tall.astype(jnp.int32) == lane // half)
        & (iota((wide, edge), 0) % half == lane % half),
        1.0,
        0.0,
    ).astype(BF16)

    for h in range(HALVES):
        exchange_wait(0, h)
        reply(1, h, combine(0, h))
        exchange_start(1, h)
    turn_tiles()
    for h in range(HALVES):
        exchange_wait(1, h)
        spread(1, h)
    forward_tiles()
    gather_rows()

    sums_ready(0, to_row(column_sums(hub_stage), 0, cols))
    set_source(lambda b: hub_stage[b * cols : (b + 1) * cols, :], True)
    steps = tile_total // (4 * QUADS)
    each = devices // steps
    for i in range(1, steps):
        sums_send(0, lax.rem(me + i * each, devices))

    def sums_beside(i):
        for u in range(1, each):
            sums_send(0, lax.rem(me + i * each + u, devices))

    transpose_tiles(0, tile_total, QUADS, True, sums_beside)
    for h in range(HALVES):
        scatter_to_slots(2, h)
        exchange_start(2, h)
    totals = sums_wait(0)
    auth_row = jnp.zeros((1, edge), F32)
    for h in range(HALVES):
        scale = inverse_norm(totals, h * half, half)
        exchange_wait(2, h)
        auth_stage[h] = combine(2, h) * jnp.concatenate([scale] * (blocks * half // cols), axis=0)
        reply(3, h, auth_stage[h])
        exchange_start(3, h)
        auth_row += to_row(column_sums(auth_stage.at[h]), cols + h * half, half)
    for h in range(HALVES):
        exchange_wait(3, h)
        spread(3, h)
    forward_tiles()
    gather_rows()
    sums_ready(1, to_row(column_sums(hub_stage), 0, cols) + auth_row)
    for offset in order:
        sums_send(1, target(offset))
    totals = sums_wait(1)
    hub_scale = inverse_norm(totals, 0, cols)
    for b in range(blocks):
        hub_out[:, b * edge : (b + 1) * edge] = hub_stage[b * cols : (b + 1) * cols, :] * hub_scale
    for h in range(HALVES):
        auth_scale = inverse_norm(totals, cols + h * half, half)
        for g in range(blocks * half // cols):
            both = auth_stage[h, g * cols : (g + 1) * cols, :] * auth_scale
            for q in range(cols // half):
                b = g * (cols // half) + q
                auth_out[h * half : (h + 1) * half, b * edge : (b + 1) * edge] = both[
                    q * half : (q + 1) * half
                ]

    wait_bytes(recv_idx, idx_send_sem)
    for which in range(2):
        wait_bytes(recv_sum.at[which], sum_send_sem.at[which])
    for phase in range(4):
        for h in range(HALVES):
            wait_bytes(recv.at[phase, h], send_sem.at[phase, h])


def finish_kernel(hub_in, auth_in, hub_out, auth_out):
    hub_out[...] = hub_in[...]
    auth_out[...] = auth_in[...]


def finish(hub, authority):
    vmem = pl.BlockSpec(memory_space=pltpu.VMEM)
    return pl.pallas_call(
        finish_kernel,
        out_shape=(jax.ShapeDtypeStruct(hub.shape, F32),) * 2,
        in_specs=[vmem] * 2,
        out_specs=(vmem, vmem),
    )(*[pltpu.with_memory_space_constraint(v, pltpu.VMEM) for v in (hub, authority)])


def per_device(edge_tiles, tile_row, tile_slot, tile_count, fetch_list, hub_start):
    devices = lax.axis_size(AXIS)
    tile_total, edge, _ = edge_tiles.shape
    cols, nodes = hub_start.shape
    blocks = nodes // edge
    slots_total = fetch_list.shape[1]
    half = cols // HALVES
    part = slots_total // devices * half
    wide = slots_total * half
    smem = pl.BlockSpec(memory_space=pltpu.SMEM)
    vmem = pl.BlockSpec(memory_space=pltpu.VMEM)
    dma = pltpu.SemaphoreType.DMA
    results = pl.pallas_call(
        functools.partial(kernel, devices, nodes * devices),
        out_shape=(pltpu.VMEM((cols, nodes), F32),) * 2,
        in_specs=[smem, smem, smem, pl.BlockSpec(memory_space=pl.ANY)] + [vmem] * 4,
        out_specs=(vmem, vmem),
        scratch_shapes=[
            pltpu.VMEM((tile_total, edge, edge), BF16),
            pltpu.VMEM((tile_total, edge, edge), BF16),
            pltpu.VMEM((cols * tile_total, edge), F32),
            pltpu.VMEM((HALVES, wide, edge), F32),
            pltpu.VMEM((slots_total, cols, edge), F32),
            pltpu.VMEM((slots_total, tile_total), BF16),
            pltpu.VMEM((wide, edge), BF16),
            pltpu.VMEM((blocks * half, wide), BF16),
        ]
        + [pltpu.VMEM((blocks, 2 * cols, edge), BF16)] * 4
        + [
            pltpu.VMEM((blocks * cols, edge), F32),
            pltpu.VMEM((HALVES, blocks * half, edge), F32),
            pltpu.VMEM((4, HALVES, devices, part, edge), BF16),
            pltpu.VMEM((4, HALVES, devices, part, edge), BF16),
            pltpu.VMEM((1, edge), F32),
            pltpu.VMEM((devices, 1, edge), F32),
            pltpu.VMEM((2, 1, edge), F32),
            pltpu.VMEM((2, devices, 1, edge), F32),
            dma((CHUNKS,)),
            dma((4, HALVES)),
            dma((4, HALVES)),
            dma,
            dma,
            dma((2,)),
            dma((2,)),
        ],
        compiler_params=pltpu.CompilerParams(
            collective_id=0, has_side_effects=True, vmem_limit_bytes=60 << 20
        ),
    )(
        tile_row,
        tile_slot,
        tile_count,
        edge_tiles,
        tile_row.reshape(1, tile_total),
        tile_slot.reshape(1, tile_total),
        fetch_list,
        hub_start,
    )
    return finish(*results)


def solution(mesh):
    placed = (P(AXIS, None, None), P(AXIS), P(AXIS), P(AXIS), P(AXIS, None), P(None, AXIS))
    return jax.shard_map(
        per_device,
        mesh=mesh,
        in_specs=placed,
        out_specs=(P(None, AXIS), P(None, AXIS)),
        check_vma=False,
    )
```

```python
import functools

import jax
import jax.numpy as jnp
import numpy as np
from jax import lax
from jax.experimental import pallas as pl
from jax.experimental.pallas import tpu as pltpu
from jax.sharding import PartitionSpec as P

AXIS = "rows"
EPS = 1e-06
F32 = jnp.float32
BF16 = jnp.bfloat16
CHUNKS = 8
QUADS = 64
TURNS = 16
HALVES = 4
GRID = (4, 4, 4, 2)
MESH = pl.DeviceIdType.MESH


def dot_nn(lhs, rhs):
    return lax.dot_general(lhs, rhs, (((1,), (0,)), ((), ())), preferred_element_type=F32)


def split_bf16(x):
    high = x.astype(BF16)
    return high, (x - high.astype(F32)).astype(BF16)


def iota(shape, dim):
    return lax.broadcasted_iota(jnp.int32, shape, dim)


def ring_distance(offset):
    return [min(o, size - o) for o, size in zip(offset[:3], GRID)]


def send_order():
    def key(offset):
        away = ring_distance(offset)
        return (-sum(d > 0 for d in away), -sum(away), offset)

    every = list(np.ndindex(*GRID))[1:]
    ordered = []
    for offset in sorted(every, key=key):
        back = tuple((size - o) % size for o, size in zip(offset[:3], GRID)) + offset[3:]
        for each in (offset, back):
            if each not in ordered:
                ordered.append(each)
    return ordered


def kernel(
    devices,
    node_total,
    rows_s,
    slots_s,
    count_s,
    tiles_hbm,
    rows_v,
    slots_v,
    fetch_v,
    hub_v,
    hub_out,
    auth_out,
    tiles,
    turned,
    prod,
    stage,
    fetched,
    onehot_slot,
    pick_t,
    pick,
    src_a,
    src_b,
    src_al,
    src_bl,
    hub_stage,
    auth_stage,
    send,
    recv,
    send_idx,
    recv_idx,
    send_sum,
    recv_sum,
    tile_sem,
    send_sem,
    recv_sem,
    idx_send_sem,
    idx_recv_sem,
    sum_send_sem,
    sum_recv_sem,
):
    tile_total, edge, _ = tiles.shape
    cols = hub_v.shape[0]
    blocks = hub_v.shape[1] // edge
    slots_total = fetch_v.shape[1]
    slots_each = slots_total // devices
    half = cols // HALVES
    part = slots_each * half
    wide = slots_total * half
    me = lax.axis_index(AXIS)
    barrier = pltpu.get_barrier_semaphore()

    order = send_order()
    place = []
    inner = 1
    for size in GRID[::-1]:
        here = lax.rem(me // inner, size)
        place.insert(0, [lax.rem(here + k, size) * inner for k in range(size)])
        inner *= size
    outer_part = [[a + b for b in place[1]] for a in place[0]]
    inner_part = [[a + b for b in place[3]] for a in place[2]]

    def target(offset):
        return outer_part[offset[0]][offset[1]] + inner_part[offset[2]][offset[3]]

    per_chunk = tile_total // CHUNKS
    for q in range(CHUNKS):
        window = pl.ds(q * per_chunk, per_chunk)
        pltpu.make_async_copy(tiles_hbm.at[window], tiles.at[window], tile_sem.at[q]).start()

    for offset in order:
        pl.semaphore_signal(barrier, inc=1, device_id=(target(offset),), device_id_type=MESH)

    zero_block = jnp.zeros((cols, edge), F32)

    def set_source(blocks_f32, with_low):
        for b in range(blocks):
            x = blocks_f32(b)
            up = jnp.concatenate([x, zero_block], axis=0)
            down = jnp.concatenate([zero_block, x], axis=0)
            if with_low:
                src_a[b], src_al[b] = split_bf16(up)
                src_b[b], src_bl[b] = split_bf16(down)
            else:
                src_a[b] = up.astype(BF16)
                src_b[b] = down.astype(BF16)

    def store_quad(t, o):
        prod[pl.ds(t, cols, stride=tile_total), :] = o[:cols, :edge]
        prod[pl.ds(t + 1, cols, stride=tile_total), :] = o[cols : 2 * cols, :edge]
        prod[pl.ds(t + 2, cols, stride=tile_total), :] = o[2 * cols : 3 * cols, edge:]
        prod[pl.ds(t + 3, cols, stride=tile_total), :] = o[3 * cols :, edge:]

    def quad_lhs(a, b, t):
        r = [rows_s[t + q] for q in range(4)]
        return jnp.concatenate(
            [
                jnp.concatenate([a[r[0]], b[r[1]]], axis=1),
                jnp.concatenate([a[r[2]], b[r[3]]], axis=1),
            ],
            axis=0,
        )

    def quad_rhs(ref, t):
        return jnp.concatenate(
            [
                ref[pl.ds(t, 2)].reshape(2 * edge, edge),
                ref[pl.ds(t + 2, 2)].reshape(2 * edge, edge),
            ],
            axis=1,
        )

    def transpose_tiles(first, total, quads, with_low, beside=None):
        def body(i, carry):
            if beside is not None:
                beside(i)
            for u in range(quads):
                t = first + (i * quads + u) * 4
                lhs = quad_lhs(src_a, src_b, t)
                if with_low:
                    lhs = jnp.concatenate([lhs, quad_lhs(src_al, src_bl, t)], axis=0)
                o = dot_nn(lhs, quad_rhs(tiles, t))
                if with_low:
                    o = o[: 4 * cols] + o[4 * cols :]
                store_quad(t, o)
            return carry

        lax.fori_loop(0, total // (4 * quads), body, 0)

    def forward_tiles():
        def body(i, carry):
            for u in range(QUADS):
                t = (i * QUADS + u) * 4
                f = [fetched[slots_s[t + q]] for q in range(4)]
                lhs = jnp.concatenate(
                    [
                        jnp.concatenate([f[0], zero_block, f[2], zero_block], axis=0),
                        jnp.concatenate([zero_block, f[1], zero_block, f[3]], axis=0),
                    ],
                    axis=1,
                ).astype(BF16)
                store_quad(t, dot_nn(lhs, quad_rhs(turned, t)))
            return carry

        lax.fori_loop(0, tile_total // (4 * QUADS), body, 0)

    def turn_tiles():
        def body(i, carry):
            for u in range(TURNS):
                t = i * TURNS + u
                turned[t] = tiles[t].T
            return carry

        lax.fori_loop(0, tile_total // TURNS, body, 0)

    def prod_split(c):
        return split_bf16(prod[c * tile_total : (c + 1) * tile_total, :])

    def scatter_to_slots(phase, h):
        chooser = onehot_slot[...]
        for c in range(half):
            high, low = prod_split(h * half + c)
            total = dot_nn(chooser, jnp.concatenate([high, low], axis=1))
            total = total[:, :edge] + total[:, edge:]
            stage[h, pl.ds(c, slots_total, stride=half), :] = total
        send[phase, h] = stage[h].astype(BF16).reshape(devices, part, edge)

    def exchange_start(phase, h):
        for offset in order:
            d = target(offset)
            pltpu.make_async_remote_copy(
                src_ref=send.at[phase, h, d],
                dst_ref=recv.at[phase, h, me],
                send_sem=send_sem.at[phase, h],
                recv_sem=recv_sem.at[phase, h],
                device_id=(d,),
                device_id_type=MESH,
            ).start()
        recv[phase, h, me] = send[phase, h, me]

    def wait_bytes(ref, sem):
        others = ref.at[pl.ds(0, devices - 1)]
        pltpu.make_async_copy(others, others, sem).wait()

    def exchange_wait(phase, h):
        wait_bytes(recv.at[phase, h], recv_sem.at[phase, h])

    def sums_send(which, d):
        pltpu.make_async_remote_copy(
            src_ref=send_sum.at[which],
            dst_ref=recv_sum.at[which, me],
            send_sem=sum_send_sem.at[which],
            recv_sem=sum_recv_sem.at[which],
            device_id=(d,),
            device_id_type=MESH,
        ).start()

    def sums_ready(which, row):
        send_sum[which] = row
        recv_sum[which, me] = row

    def sums_wait(which):
        wait_bytes(recv_sum.at[which], sum_recv_sem.at[which])
        return jnp.sum(recv_sum[which], axis=0)

    def to_row(column, offset, period):
        spot = iota((cols, edge), 1) == iota((cols, edge), 0) % period + offset
        return jnp.sum(jnp.where(spot, column, 0.0), axis=0, keepdims=True)

    def to_column(row, offset, period):
        spot = iota((cols, edge), 1) == iota((cols, edge), 0) % period + offset
        return jnp.sum(jnp.where(spot, row, 0.0), axis=1, keepdims=True)

    def inverse_norm(row, offset, period):
        return 1.0 / jnp.sqrt(to_column(row, offset, period) / node_total + EPS)

    def combine(phase, h):
        return dot_nn(pick[...], recv[phase, h].reshape(wide, edge))

    def reply(phase, h, authority):
        low = authority.astype(BF16)
        low = jnp.concatenate([low, jnp.zeros((edge - blocks * half, edge), BF16)], axis=0)
        answer = dot_nn(pick_t[...], low).astype(BF16)
        send[phase, h] = answer.reshape(devices, part, edge)

    def gather_rows():
        alive = iota((blocks, tile_total), 1) < count_s[0]
        chooser = jnp.where(
            alive & (rows_v[...] == iota((blocks, tile_total), 0)), 1.0, 0.0
        ).astype(BF16)
        for c in range(cols):
            high, low = prod_split(c)
            total = dot_nn(chooser, high) + dot_nn(chooser, low)
            hub_stage[pl.ds(c, blocks, stride=cols), :] = total

    def column_sums(ref):
        total = jnp.zeros((cols, edge), F32)
        for g in range(ref.shape[0] // cols):
            x = ref[g * cols : (g + 1) * cols, :]
            total = total + x * x
        return jnp.sum(total, axis=1, keepdims=True)

    def spread(phase, h):
        arrived = recv[phase, h].reshape(wide, edge).astype(F32)
        fetched[:, h * half : (h + 1) * half, :] = arrived.reshape(slots_total, half, edge)

    set_source(lambda b: hub_v[:, b * edge : (b + 1) * edge], False)
    alive = iota((slots_total, tile_total), 1) < count_s[0]
    onehot_slot[...] = jnp.where(
        alive & (slots_v[...] == iota((slots_total, tile_total), 0)), 1.0, 0.0
    ).astype(BF16)
    for q in range(CHUNKS):
        window = pl.ds(q * per_chunk, per_chunk)
        pltpu.make_async_copy(tiles_hbm.at[window], tiles.at[window], tile_sem.at[q]).wait()
        transpose_tiles(q * per_chunk, per_chunk, per_chunk // 4, False)
    for h in range(HALVES):
        scatter_to_slots(0, h)
    index = iota((slots_total, edge), 0)
    weight = jnp.where(index % slots_each == 0, 1.0, 1.0 * blocks)
    packer = jnp.where(index // slots_each == iota((slots_total, edge), 1), weight, 0.0)
    list_row = jnp.broadcast_to(fetch_v[...].astype(F32), (cols, slots_total))
    list_row = dot_nn(list_row.astype(BF16), packer.astype(BF16))[:1]
    send_idx[...] = list_row
    pl.semaphore_wait(barrier, devices - 1)

    for offset in order:
        d = target(offset)
        pltpu.make_async_remote_copy(
            src_ref=send_idx,
            dst_ref=recv_idx.at[me],
            send_sem=idx_send_sem,
            recv_sem=idx_recv_sem,
            device_id=(d,),
            device_id_type=MESH,
        ).start()
    recv_idx[me] = list_row
    for h in range(HALVES):
        exchange_start(0, h)

    wait_bytes(recv_idx, idx_recv_sem)
    lists = recv_idx[...].reshape(devices, edge)
    pair = jnp.sum(jnp.where(iota((devices, edge), 1) == me, lists, 0.0), axis=1, keepdims=True)
    pair = jnp.broadcast_to(pair, (devices, edge)).astype(jnp.int32)
    columns = [(pair % blocks).astype(F32), (pair // blocks).astype(F32)]
    line = jnp.zeros((cols, wide), F32)
    tall = jnp.zeros((wide, edge), F32)
    for k in range(slots_each):
        j = iota((devices, wide), 1)
        p = iota((devices, wide), 0)
        expand = jnp.where((j // part == p) & ((j // half) % slots_each == k), 1.0, 0.0)
        line = line + dot_nn(columns[k].T[:cols].astype(BF16), expand.astype(BF16))
        j = iota((wide, devices), 0)
        p = iota((wide, devices), 1)
        expand = jnp.where((j // part == p) & ((j // half) % slots_each == k), 1.0, 0.0)
        tall = tall + dot_nn(expand.astype(BF16), columns[k].astype(BF16))
    line_blocks = line.astype(jnp.int32)
    row = iota((cols, wide), 0)
    same = iota((cols, wide), 1) % half == row % half
    for b in range(0, blocks, 4):
        pick[b * half : (b + 4) * half, :] = jnp.concatenate(
            [
                jnp.where((line_blocks == b + g + row // half) & same, 1.0, 0.0)
                for g in range(0, 4, cols // half)
            ],
            axis=0,
        ).astype(BF16)
    lane = iota((wide, edge), 1)
    pick_t[...] = jnp.where(
        (tall.astype(jnp.int32) == lane // half)
        & (iota((wide, edge), 0) % half == lane % half),
        1.0,
        0.0,
    ).astype(BF16)

    for h in range(HALVES):
        exchange_wait(0, h)
        reply(1, h, combine(0, h))
        exchange_start(1, h)
    turn_tiles()
    for h in range(HALVES):
        exchange_wait(1, h)
        spread(1, h)
    forward_tiles()
    gather_rows()

    sums_ready(0, to_row(column_sums(hub_stage), 0, cols))
    set_source(lambda b: hub_stage[b * cols : (b + 1) * cols, :], True)
    steps = tile_total // (4 * QUADS)
    each = devices // steps
    for i in range(1, steps):
        sums_send(0, lax.rem(me + i * each, devices))

    def sums_beside(i):
        for u in range(1, each):
            sums_send(0, lax.rem(me + i * each + u, devices))

    transpose_tiles(0, tile_total, QUADS, True, sums_beside)
    for h in range(HALVES):
        scatter_to_slots(2, h)
        exchange_start(2, h)
    totals = sums_wait(0)
    auth_row = jnp.zeros((1, edge), F32)
    for h in range(HALVES):
        scale = inverse_norm(totals, h * half, half)
        exchange_wait(2, h)
        auth_stage[h] = combine(2, h) * jnp.concatenate([scale] * (blocks * half // cols), axis=0)
        reply(3, h, auth_stage[h])
        exchange_start(3, h)
        auth_row += to_row(column_sums(auth_stage.at[h]), cols + h * half, half)
    for h in range(HALVES):
        exchange_wait(3, h)
        spread(3, h)
    forward_tiles()
    gather_rows()
    sums_ready(1, to_row(column_sums(hub_stage), 0, cols) + auth_row)
    for offset in order:
        sums_send(1, target(offset))
    totals = sums_wait(1)
    hub_scale = inverse_norm(totals, 0, cols)
    for b in range(blocks):
        hub_out[:, b * edge : (b + 1) * edge] = hub_stage[b * cols : (b + 1) * cols, :] * hub_scale
    for h in range(HALVES):
        auth_scale = inverse_norm(totals, cols + h * half, half)
        for g in range(blocks * half // cols):
            both = auth_stage[h, g * cols : (g + 1) * cols, :] * auth_scale
            for q in range(cols // half):
                b = g * (cols // half) + q
                auth_out[h * half : (h + 1) * half, b * edge : (b + 1) * edge] = both[
                    q * half : (q + 1) * half
                ]

    wait_bytes(recv_idx, idx_send_sem)
    for which in range(2):
        wait_bytes(recv_sum.at[which], sum_send_sem.at[which])
    for phase in range(4):
        for h in range(HALVES):
            wait_bytes(recv.at[phase, h], send_sem.at[phase, h])


def finish_kernel(hub_in, auth_in, hub_out, auth_out):
    hub_out[...] = hub_in[...]
    auth_out[...] = auth_in[...]


def finish(hub, authority):
    vmem = pl.BlockSpec(memory_space=pltpu.VMEM)
    return pl.pallas_call(
        finish_kernel,
        out_shape=(jax.ShapeDtypeStruct(hub.shape, F32),) * 2,
        in_specs=[vmem] * 2,
        out_specs=(vmem, vmem),
    )(*[pltpu.with_memory_space_constraint(v, pltpu.VMEM) for v in (hub, authority)])


def per_device(edge_tiles, tile_row, tile_slot, tile_count, fetch_list, hub_start):
    devices = lax.axis_size(AXIS)
    tile_total, edge, _ = edge_tiles.shape
    cols, nodes = hub_start.shape
    blocks = nodes // edge
    slots_total = fetch_list.shape[1]
    half = cols // HALVES
    part = slots_total // devices * half
    wide = slots_total * half
    smem = pl.BlockSpec(memory_space=pltpu.SMEM)
    vmem = pl.BlockSpec(memory_space=pltpu.VMEM)
    dma = pltpu.SemaphoreType.DMA
    results = pl.pallas_call(
        functools.partial(kernel, devices, nodes * devices),
        out_shape=(pltpu.VMEM((cols, nodes), F32),) * 2,
        in_specs=[smem, smem, smem, pl.BlockSpec(memory_space=pl.ANY)] + [vmem] * 4,
        out_specs=(vmem, vmem),
        scratch_shapes=[
            pltpu.VMEM((tile_total, edge, edge), BF16),
            pltpu.VMEM((tile_total, edge, edge), BF16),
            pltpu.VMEM((cols * tile_total, edge), F32),
            pltpu.VMEM((HALVES, wide, edge), F32),
            pltpu.VMEM((slots_total, cols, edge), F32),
            pltpu.VMEM((slots_total, tile_total), BF16),
            pltpu.VMEM((wide, edge), BF16),
            pltpu.VMEM((blocks * half, wide), BF16),
        ]
        + [pltpu.VMEM((blocks, 2 * cols, edge), BF16)] * 4
        + [
            pltpu.VMEM((blocks * cols, edge), F32),
            pltpu.VMEM((HALVES, blocks * half, edge), F32),
            pltpu.VMEM((4, HALVES, devices, part, edge), BF16),
            pltpu.VMEM((4, HALVES, devices, part, edge), BF16),
            pltpu.VMEM((1, edge), F32),
            pltpu.VMEM((devices, 1, edge), F32),
            pltpu.VMEM((2, 1, edge), F32),
            pltpu.VMEM((2, devices, 1, edge), F32),
            dma((CHUNKS,)),
            dma((4, HALVES)),
            dma((4, HALVES)),
            dma,
            dma,
            dma((2,)),
            dma((2,)),
        ],
        compiler_params=pltpu.CompilerParams(
            collective_id=0, has_side_effects=True, vmem_limit_bytes=60 << 20
        ),
    )(
        tile_row,
        tile_slot,
        tile_count,
        edge_tiles,
        tile_row.reshape(1, tile_total),
        tile_slot.reshape(1, tile_total),
        fetch_list,
        hub_start,
    )
    return finish(*results)


def solution(mesh):
    placed = (P(AXIS, None, None), P(AXIS), P(AXIS), P(AXIS), P(AXIS, None), P(None, AXIS))
    return jax.shard_map(
        per_device,
        mesh=mesh,
        in_specs=placed,
        out_specs=(P(None, AXIS), P(None, AXIS)),
        check_vma=False,
    )
```
